256 devices in a mesh: leaf: 64 (over z, x, core), level: 4 (over y).
Axes of the slice: x: 4, y: 4, z: 8, core: 2. Of those that a mesh axis runs over, the one named last changes fastest.
Arguments:
- charges: bfloat16 [3072, 128, 256], P(('leaf', 'level')), may hold values from -6 to 6
- near_mat: bfloat16 [3072, 16, 128, 128], P(('leaf', 'level')), may hold values from -0.1875 to 0.1875
- near_source: int32 [3072, 16], P(('leaf', 'level')), may hold values from 0 to 143
- near_count: int32 [3072], P(('leaf', 'level')), may hold values from 1 to 16, as said below
- moment_map: bfloat16 [3072, 256, 128], P(('leaf', 'level')), may hold values from -0.078125 to 0.078125
- local_eval: bfloat16 [3072, 128, 256], P(('leaf', 'level')), may hold values from -0.375 to 0.375
- upward_child_translation: bfloat16 [8, 256, 256], replicated, may hold values from -0.125 to 0.125
- shift_down: bfloat16 [8, 256, 256], replicated, may hold values from -0.375 to 0.375
- transfer_ops: bfloat16 [8, 256, 256], replicated, may hold values from -0.0625 to 0.0625
- subtree_interaction_list: int32 [64, 32], P('leaf'), may hold values from 0 to 63
- subtree_interaction_operators: int32 [64, 32], P('leaf'), may hold values from 0 to 7
- parent_list: int32 [64, 8], P('leaf'), may hold values from 0 to 7
- parent_ops: int32 [64, 8], P('leaf'), may hold values from 0 to 7
Outputs:
- potential: float32 [3072, 128, 256], P(('leaf', 'level'))
The draws below stay inside these ranges and needn't reach their ends.
Inputs may be any that keep to these rules, and one draw needn't show every extreme that they name: `near_count`: some block uses all 16 slots and some block only one.
All inputs are finite; a program needn't handle non-finite values.
Results may differ from the reference program's by a relative error of at most 0.012.
Values may be sent and summed in bfloat16 or wider, within the bound.
No kernel may reach another device: no remote copies, remote signals or barrier semaphores. Data moves between devices by JAX's collectives and lax.ppermute only.
A program may use at most 128 MiB of HBM per device.

```python
import jax
import jax.numpy as jnp
from jax import lax

P_SIZE = 128
C = 256
R = 256
NEAR = 16
K0 = 32
K1 = 8
NOPS = 8
SUB = 48
NBLK = 3072
LEAVES = 64
PARENTS = 8


def draw_near_count(key, part):
    values = jax.random.randint(key, (NBLK,), 1, NEAR + 1)
    values = values.at[0].set(NEAR)
    values = values.at[1].set(1)
    return values.astype(jnp.int32)


def place_ends(entries, own_key, smallest, largest):
    longest = entries.shape.index(max(entries.shape))
    spots = []
    for shift in (0, 1):
        where = [jax.random.randint(jax.random.fold_in(own_key, axis), (), 0, length) for axis, length in enumerate(entries.shape)]
        where[longest] = (where[longest] + shift) % entries.shape[longest]
        spots.append(tuple(where))
    return entries.at[spots[0]].set(smallest).at[spots[1]].set(largest)


def block_scale(rng, extent, cuts, least, largest):
    loudness = 1.0
    for axis_at, shards_of in cuts:
        heights = jax.random.uniform(jax.random.fold_in(jax.random.fold_in(rng, 6), axis_at), (shards_of,), jnp.float32, least / len(cuts), largest / len(cuts))
        loudness = loudness * jnp.repeat(jnp.exp(heights), extent[axis_at] // shards_of).reshape((-1,) + (1,) * (len(extent) - 1 - axis_at))
    return loudness


def noise(rng, shape, deviation, reach, cuts=(), kind=jnp.bfloat16):
    loudness = block_scale(rng, shape, cuts, -0.22, 0.18) if cuts else 1.0
    array = jax.random.normal(rng, shape, jnp.float32) * deviation * loudness
    return jnp.minimum(jnp.maximum(array, -reach), reach).astype(kind)


def setup_inputs(seed: int = 0) -> dict:
    arg_keys = jax.random.split(jax.random.key(seed), 14)
    charges = noise(arg_keys[0], (NBLK, P_SIZE, R), 1.0, 6.0, ((0, 256),))
    near_mat = noise(arg_keys[1], (NBLK, NEAR, P_SIZE, P_SIZE), (P_SIZE * NEAR // 2) ** -0.5, 0.1875, ((0, 256),))
    near_source = place_ends(jax.random.randint(arg_keys[2], (NBLK, NEAR), 0, 3 * SUB), jax.random.fold_in(arg_keys[2], 1), 0, (3 * SUB) - 1).astype(jnp.int32)
    near_count = draw_near_count(jax.random.fold_in(arg_keys[13], 71), 0)
    moment_map = noise(arg_keys[4], (NBLK, C, P_SIZE), (P_SIZE * SUB) ** -0.5, 0.078125, ((0, 256),))
    local_eval = noise(arg_keys[5], (NBLK, P_SIZE, C), C ** -0.5, 0.375, ((0, 256),))
    upward_child_translation = noise(arg_keys[6], (8, C, C), (8 * C) ** -0.5, 0.125)
    shift_down = noise(arg_keys[7], (8, C, C), C ** -0.5, 0.375)
    transfer_ops = noise(arg_keys[8], (NOPS, C, C), (C * K0) ** -0.5, 0.0625)
    subtree_interaction_list = place_ends(jax.random.randint(arg_keys[9], (LEAVES, K0), 0, LEAVES), jax.random.fold_in(arg_keys[9], 1), 0, LEAVES - 1).astype(jnp.int32)
    subtree_interaction_operators = place_ends(jax.random.randint(arg_keys[10], (LEAVES, K0), 0, NOPS), jax.random.fold_in(arg_keys[10], 1), 0, NOPS - 1).astype(jnp.int32)
    parent_list = place_ends(jax.random.randint(arg_keys[11], (LEAVES, K1), 0, PARENTS), jax.random.fold_in(arg_keys[11], 1), 0, PARENTS - 1).astype(jnp.int32)
    parent_ops = place_ends(jax.random.randint(arg_keys[12], (LEAVES, K1), 0, NOPS), jax.random.fold_in(arg_keys[12], 1), 0, NOPS - 1).astype(jnp.int32)
    return {"charges": charges, "near_mat": near_mat, "near_source": near_source, "near_count": near_count, "moment_map": moment_map, "local_eval": local_eval, "upward_child_translation": upward_child_translation, "shift_down": shift_down, "transfer_ops": transfer_ops, "subtree_interaction_list": subtree_interaction_list, "subtree_interaction_operators": subtree_interaction_operators, "parent_list": parent_list, "parent_ops": parent_ops}


def reference(charges, near_mat, near_source, near_count, moment_map, local_eval, upward_child_translation, shift_down, transfer_ops, subtree_interaction_list, subtree_interaction_operators, parent_list, parent_ops):
    single_precision = jnp.float32
    zero_padding_rows = jnp.zeros((SUB, P_SIZE, R), jnp.bfloat16)
    padded = jnp.concatenate([zero_padding_rows, charges, zero_padding_rows], 0)
    mats = near_mat.reshape(LEAVES, SUB, NEAR, P_SIZE, P_SIZE)
    sources = near_source.reshape(LEAVES, SUB, NEAR)
    counts = near_count.reshape(LEAVES, SUB)

    def near_one(piece_collection):
        block_mat, block_src, block_cnt, leaf_index = piece_collection
        window = lax.dynamic_slice_in_dim(padded, (leaf_index * SUB).astype(jnp.int32), 3 * SUB, 0)
        picked = window[block_src].astype(single_precision)
        active = (jnp.arange(NEAR, dtype=jnp.int32)[None, :] < block_cnt[:, None]).astype(single_precision)
        picked = picked * active[:, :, None, None]
        return jnp.einsum('bkpq,bkqr->bpr', block_mat.astype(single_precision), picked)

    near_part = lax.map(near_one, (mats, sources, counts, jnp.arange(LEAVES, dtype=jnp.int32)))

    def moment_one(piece_collection):
        maps, block_charges = piece_collection
        return jnp.einsum('bcp,bpr->cr', maps.astype(single_precision), block_charges.astype(single_precision)).astype(jnp.bfloat16)

    moments = lax.map(moment_one, (moment_map.reshape(LEAVES, SUB, C, P_SIZE), charges.reshape(LEAVES, SUB, P_SIZE, R)))
    grouped_terms = moments.reshape(PARENTS, 8, C, R)
    upper_levels = jnp.einsum('get,kgtv->kev', upward_child_translation.astype(single_precision), grouped_terms.astype(single_precision)).astype(jnp.bfloat16)

    def local_one(piece_collection):
        leaf_ids, leaf_kinds, parent_ids, parent_kinds, leaf_index = piece_collection
        far_leaf = jnp.einsum('kcd,kdr->cr', transfer_ops[leaf_kinds].astype(single_precision), moments[leaf_ids].astype(single_precision))
        coarse = jnp.einsum('kcd,kdr->cr', transfer_ops[parent_kinds].astype(single_precision), upper_levels[parent_ids].astype(single_precision)).astype(jnp.bfloat16)
        downward = jnp.dot(shift_down[leaf_index % 8], coarse, preferred_element_type=jnp.float32)
        return (far_leaf + downward).astype(jnp.bfloat16)

    local = lax.map(local_one, (subtree_interaction_list, subtree_interaction_operators, parent_list, parent_ops, jnp.arange(LEAVES, dtype=jnp.int32)))

    def far_one(piece_collection):
        evals, expansion = piece_collection
        return jnp.einsum('bpc,cr->bpr', evals.astype(single_precision), expansion.astype(single_precision))

    far_part = lax.map(far_one, (local_eval.reshape(LEAVES, SUB, P_SIZE, C), local))
    return (near_part + far_part).reshape(NBLK, P_SIZE, R)
```

```python
import jax
import jax.numpy as jnp
from jax import lax
from jax.experimental import pallas as pl
from jax.experimental.pallas import tpu as pltpu
from jax.sharding import PartitionSpec as P


BOTH = ("leaf", "level")
NT = (((1,), (1,)), ((), ()))
F32 = jnp.float32
BF16 = jnp.bfloat16


def dot(a, b):
    return jnp.dot(a, b, preferred_element_type=F32)


def dot_nt(a, b):
    return lax.dot_general(a, b, NT, preferred_element_type=F32)


def moment_kernel(charges, maps, cells, ops, parents, parent_ops, out, row):
    blocks = charges.shape[0]
    total = None
    for b in range(0, blocks, 2):
        left = jnp.concatenate([maps[b], maps[b + 1]], axis=1)
        right = jnp.concatenate([charges[b], charges[b + 1]], axis=0)
        part = dot(left, right)
        total = part if total is None else total + part
    total = total.astype(BF16)
    row[...] = jnp.zeros_like(row)
    row[0:1, 0:32] = ((cells[...] & 7) * 8 + (cells[...] >> 3)).astype(F32)
    row[0:1, 32:64] = ops[...].astype(F32)
    row[0:1, 64:72] = parents[...].astype(F32)
    row[0:1, 72:80] = parent_ops[...].astype(F32)
    rows, cols = iota((1024, 512), 0), iota((1024, 512), 1)
    spread = jnp.where(rows == (cols & 255) * 4 + (cols >> 8), 1.0, 0.0).astype(BF16)
    parts = dot_nt(spread, jnp.concatenate([total[0:128], total[128:256]], axis=1))
    lists = jnp.broadcast_to(row[0:1, :], (1024, 128))
    out[...] = jnp.where((iota((1024, 128), 0) & 3) == 2, lists, parts).astype(BF16)


def iota(shape, dim):
    return lax.broadcasted_iota(jnp.int32, shape, dim)


def split(x):
    high = x.astype(BF16)
    return high, (x - high.astype(F32)).astype(BF16)


def far_kernel(received, upward_hbm, transfer_hbm, shift_hbm, out, upward, transfer, shift, sems):
    pairs = ((upward_hbm, upward), (transfer_hbm, transfer), (shift_hbm, shift))
    copies = [pltpu.make_async_copy(a, b, sems.at[n]) for n, (a, b) in enumerate(pairs)]
    for copy in copies:
        copy.start()
    rows, cols = iota((64, 1024), 0), iota((64, 1024), 1)
    cell = (rows & 7) * 8 + (rows >> 3)
    chosen = []
    for j in range(2):
        chosen.append(jnp.where(((cols >> 4) == cell) & ((cols & 3) == j), 1.0, 0.0))
    chosen.append(jnp.where(cols == cell * 16 + 2, 1.0, 0.0))
    gathered = dot(jnp.concatenate(chosen, axis=0).astype(BF16), received[...])
    moments = jnp.concatenate([gathered[0:64], gathered[64:128]], axis=1).astype(BF16)
    lists = gathered[128:192]
    lane = iota((64, 128), 1).astype(F32)

    codes = lists[:, 32:64] * 64.0 + lists[:, 0:32]
    counts = [jnp.zeros((64, 128), F32) for _ in range(4)]
    for k in range(32):
        code = jnp.broadcast_to(codes[:, k : k + 1], (64, 128)) - lane
        for g in range(4):
            counts[g] = counts[g] + jnp.where(code == 128.0 * g, 1.0, 0.0)
    parent_codes = lists[:, 72:80] * 8.0 + lists[:, 64:72]
    parent_counts = jnp.zeros((64, 128), F32)
    for k in range(8):
        code = jnp.broadcast_to(parent_codes[:, k : k + 1], (64, 128))
        parent_counts = parent_counts + jnp.where(code == lane, 1.0, 0.0)

    first = lane < 64.0
    picks = []
    for g in range(4):
        picks.append(jnp.where(first, counts[g], 0.0))
        picks.append(jnp.where(first, 0.0, counts[g]))
    picks = jnp.concatenate(picks, axis=0).astype(BF16)
    sums = dot(picks, jnp.concatenate([moments, moments], axis=0))
    high, low = split(sums)

    for copy in copies:
        copy.wait()
    wide = moments.astype(F32)
    upper = jnp.zeros((8, 256), F32)
    for i in range(8):
        upper = upper + dot_nt(wide[8 * i : 8 * i + 8].astype(BF16), upward[i])
    upper = upper.astype(BF16)

    far = jnp.zeros((64, 256), F32)
    moved = []
    for o in range(8):
        both = jnp.concatenate([high[64 * o : 64 * o + 64], low[64 * o : 64 * o + 64]], axis=0)
        part = dot_nt(both, transfer[o])
        far = far + part[0:64] + part[64:128]
        moved.append(dot_nt(upper, transfer[o]))
    moved_high, moved_low = split(jnp.concatenate(moved, axis=0))
    weights = parent_counts[:, 0:64].astype(BF16)
    coarse = dot(weights, moved_high) + dot(weights, moved_low)
    coarse = coarse.astype(BF16).astype(F32)
    down = [dot_nt(coarse[8 * j : 8 * j + 8].astype(BF16), shift[j]) for j in range(8)]
    local = (far + jnp.concatenate(down, axis=0)).astype(BF16)

    rows, cols = iota((512, 128), 0), iota((512, 128), 1)
    cell = (cols & 7) * 8 + ((cols >> 3) & 7)
    spread = jnp.where(((rows >> 3) == cell) & ((rows & 1) == (cols >> 6)), 1.0, 0.0).astype(BF16)
    out[...] = dot(spread, jnp.concatenate([local[:, 0:128], local[:, 128:256]], axis=0)).astype(BF16)


def panel_kernel(sources, counts, *refs):
    buffers, (mats, evals, local, out, window, turned, sems) = refs[:-7], refs[-7:]
    b = pl.program_id(0)

    @pl.when(b == 0)
    def _():
        copies = []
        for n, buffer in enumerate(buffers):
            copies.append(pltpu.make_async_copy(buffer, window.at[pl.ds(n * 12, 12)], sems.at[n]))
        for copy in copies:
            copy.start()
        rows, cols = iota((512, 512), 0), iota((512, 512), 1)
        order = jnp.where(rows == (cols & 255) * 2 + (cols >> 8), 1.0, 0.0).astype(BF16)
        both = lax.dot_general(local[...], order, (((0,), (0,)), ((), ())), preferred_element_type=F32)
        turned[0:128, :] = both[:, 0:256].astype(BF16)
        turned[128:256, :] = both[:, 256:512].astype(BF16)
        for copy in copies:
            copy.wait()

    count = counts[b]

    def pair(k):
        left = jnp.concatenate(
            [
                jnp.where(k < count, mats[0, k], 0).astype(BF16),
                jnp.where(k + 1 < count, mats[0, k + 1], 0).astype(BF16),
            ],
            axis=1,
        )
        right = jnp.concatenate([window[sources[b * 16 + k]], window[sources[b * 16 + k + 1]]], axis=0)
        return dot(left, right)

    total = dot(evals[0], turned[...])
    for k in range(0, 8, 2):
        total = total + pair(k)
    out[0] = total

    @pl.when(count > 8)
    def _():
        more = pair(8)
        for k in range(10, 16, 2):
            more = more + pair(k)
        out[0] = out[0] + more


def call_moment(*args):
    return pl.pallas_call(
        moment_kernel,
        out_shape=jax.ShapeDtypeStruct((1024, 128), BF16),
        scratch_shapes=[pltpu.VMEM((8, 128), F32)],
        name="moment",
    )(*args)


def call_far(received, *weights):
    return pl.pallas_call(
        far_kernel,
        out_shape=jax.ShapeDtypeStruct((512, 128), BF16),
        in_specs=[pl.BlockSpec(memory_space=pltpu.VMEM)] + [pl.BlockSpec(memory_space=pltpu.HBM)] * 3,
        scratch_shapes=[pltpu.VMEM(w.shape, BF16) for w in weights] + [pltpu.SemaphoreType.DMA((3,))],
        compiler_params=pltpu.CompilerParams(vmem_limit_bytes=60 << 20),
        name="far",
    )(received, *weights)


def call_panel(sources, counts, buffers, mats, evals, local):
    blocks = mats.shape[0]
    total = sum(x.shape[0] for x in buffers)
    return pl.pallas_call(
        panel_kernel,
        out_shape=jax.ShapeDtypeStruct((blocks, 128, 256), F32),
        grid_spec=pltpu.PrefetchScalarGridSpec(
            num_scalar_prefetch=2,
            grid=(blocks,),
            in_specs=[pl.BlockSpec(memory_space=pltpu.HBM)] * len(buffers)
            + [
                pl.BlockSpec((1, 16, 128, 128), lambda b, *_: (b, 0, 0, 0)),
                pl.BlockSpec((1, 128, 256), lambda b, *_: (b, 0, 0)),
                pl.BlockSpec((512, 128), lambda b, *_: (0, 0)),
            ],
            out_specs=pl.BlockSpec((1, 128, 256), lambda b, *_: (b, 0, 0)),
            scratch_shapes=[
                pltpu.VMEM((total, 128, 256), BF16),
                pltpu.VMEM((256, 256), BF16),
                pltpu.SemaphoreType.DMA((len(buffers),)),
            ],
        ),
        compiler_params=pltpu.CompilerParams(vmem_limit_bytes=56 << 20),
        name="panel",
    )(sources, counts, *buffers, mats, evals, local)


def flat(pairs):
    return [(a * 4 + b, c * 4 + d) for (a, b), (c, d) in pairs]


def outer(leaf):
    return leaf + 1 if leaf % 2 else leaf - 1


def outer_pairs(leaves, turn):
    return flat(
        [
            ((leaf, y), (outer(leaf), (y + turn) % 4))
            for leaf in range(leaves)
            for y in range(4)
            if 0 <= outer(leaf) < leaves
        ]
    )


def inner_pairs(leaves):
    return flat([((leaf, y), (leaf ^ 1, y)) for leaf in range(leaves) for y in range(4)])


def on_device(
    charges,
    near_mat,
    near_source,
    near_count,
    moment_map,
    local_eval,
    upward_child_translation,
    shift_down,
    transfer_ops,
    subtree_interaction_list,
    subtree_interaction_operators,
    parent_list,
    parent_ops,
):
    leaves = lax.axis_size("leaf")
    leaf, level = lax.axis_index("leaf"), lax.axis_index("level")
    ring = [(i, (i + 1) % 4) for i in range(4)]
    back = [((i + 1) % 4, i) for i in range(4)]
    inner = inner_pairs(leaves)

    below = lax.ppermute(charges, "level", ring)
    above = lax.ppermute(charges, "level", back)
    outer_own = lax.ppermute(charges, BOTH, outer_pairs(leaves, 0))
    inner_own = lax.ppermute(charges, BOTH, inner)

    lists = (subtree_interaction_list, subtree_interaction_operators, parent_list, parent_ops)
    message = call_moment(charges, moment_map, *lists)
    received = lax.all_to_all(message.reshape(256, 4, 128), BOTH, 0, 0, tiled=True).reshape(1024, 128)

    received, below, above, outer_own = lax.optimization_barrier((received, below, above, outer_own))
    outer_below = lax.ppermute(below, BOTH, outer_pairs(leaves, 0))
    outer_above = lax.ppermute(above, BOTH, outer_pairs(leaves, 0))
    far_own = lax.ppermute(below, "level", ring)
    outer_far = lax.ppermute(above, BOTH, outer_pairs(leaves, -1))
    inner_below = lax.ppermute(below, BOTH, inner)
    inner_above = lax.ppermute(above, BOTH, inner)

    columns = call_far(received, upward_child_translation, transfer_ops, shift_down)
    local = lax.all_to_all(columns.reshape(256, 2, 128), BOTH, 0, 0, tiled=True).reshape(512, 128)

    local, far_own = lax.optimization_barrier((local, far_own))
    inner_far = lax.ppermute(far_own, BOTH, inner)

    buffers = [
        charges, above, far_own, below,
        inner_own, inner_above, inner_far, inner_below,
        outer_own, outer_above, outer_far, outer_below,
    ]
    subtree, place = near_source // 48, near_source % 48
    turn = (place // 12 - level) & 3
    odd = leaf & 1
    group = jnp.where(subtree == 1, 0, jnp.where((subtree == 0) == (odd == 1), 1, 2))
    sources = (group * 48 + turn * 12 + place % 12).reshape(-1)
    return call_panel(sources, near_count, buffers, near_mat, local_eval, local)


def solution(mesh):
    placed = (
        P(("leaf", "level"), None, None),
        P(("leaf", "level"), None, None, None),
        P(("leaf", "level"), None),
        P(("leaf", "level")),
        P(("leaf", "level"), None, None),
        P(("leaf", "level"), None, None),
        P(),
        P(),
        P(),
        P("leaf", None),
        P("leaf", None),
        P("leaf", None),
        P("leaf", None),
    )
    return jax.shard_map(
        on_device,
        mesh=mesh,
        in_specs=placed,
        out_specs=P(("leaf", "level"), None, None),
        check_vma=False,
    )
```

```python
import functools

import jax
import jax.numpy as jnp
from jax import lax
from jax.experimental import pallas as pl
from jax.experimental.pallas import tpu as pltpu
from jax.sharding import PartitionSpec as P


BOTH = ("leaf", "level")
NT = (((1,), (1,)), ((), ()))
F32 = jnp.float32
BF16 = jnp.bfloat16
GROUP = 4


def dot(a, b):
    return jnp.dot(a, b, preferred_element_type=F32)


def dot_nt(a, b):
    return lax.dot_general(a, b, NT, preferred_element_type=F32)


def moment_kernel(charges, maps, cells, ops, parents, parent_ops, *refs):
    weights, out, kept, (row, spread, sems) = refs[0:3], refs[3], refs[4:7], refs[7:]
    copies = [pltpu.make_async_copy(a, b, sems.at[n]) for n, (a, b) in enumerate(zip(weights, kept))]
    for copy in copies:
        copy.start()
    blocks = charges.shape[0]
    total = None
    for b in range(0, blocks, 2):
        left = jnp.concatenate([maps[b], maps[b + 1]], axis=1)
        right = jnp.concatenate([charges[b], charges[b + 1]], axis=0)
        part = dot(left, right)
        total = part if total is None else total + part
    turned = total.T
    row[...] = jnp.zeros_like(row)
    row[0:1, 0:32] = ((cells[...] & 7) * 8 + (cells[...] >> 3)).astype(F32)
    row[0:1, 32:64] = ops[...].astype(F32)
    row[0:1, 64:72] = parents[...].astype(F32)
    row[0:1, 72:80] = parent_ops[...].astype(F32)
    for j in range(2):
        spread[pl.ds(j, 256, stride=4), :] = turned[:, 128 * j : 128 * j + 128]
    spread[pl.ds(2, 256, stride=4), :] = jnp.broadcast_to(row[0:1, :], (256, 128))
    spread[pl.ds(3, 256, stride=4), :] = jnp.zeros((256, 128), F32)
    out[...] = spread[...].astype(BF16)
    for copy in copies:
        copy.wait()


def iota(shape, dim):
    return lax.broadcasted_iota(jnp.int32, shape, dim)


def split(x):
    high = x.astype(BF16)
    return high, (x - high.astype(F32)).astype(BF16)


def far_kernel(received, upward, transfer, shift, out):
    rows, cols = iota((64, 1024), 0), iota((64, 1024), 1)
    cell = (rows & 7) * 8 + (rows >> 3)
    chosen = []
    for j in range(2):
        chosen.append(jnp.where(((cols >> 4) == cell) & ((cols & 3) == j), 1.0, 0.0))
    chosen.append(jnp.where(cols == cell * 16 + 2, 1.0, 0.0))
    gathered = dot(jnp.concatenate(chosen, axis=0).astype(BF16), received[...])
    moments = jnp.concatenate([gathered[0:64], gathered[64:128]], axis=1).astype(BF16)
    lists = gathered[128:192]
    lane = iota((64, 128), 1).astype(F32)

    codes = lists[:, 32:64] * 64.0 + lists[:, 0:32]
    counts = [jnp.zeros((64, 128), F32) for _ in range(4)]
    for k in range(32):
        code = jnp.broadcast_to(codes[:, k : k + 1], (64, 128)) - lane
        for g in range(4):
            counts[g] = counts[g] + jnp.where(code == 128.0 * g, 1.0, 0.0)
    parent_codes = lists[:, 72:80] * 8.0 + lists[:, 64:72]
    parent_counts = jnp.zeros((64, 128), F32)
    for k in range(8):
        code = jnp.broadcast_to(parent_codes[:, k : k + 1], (64, 128))
        parent_counts = parent_counts + jnp.where(code == lane, 1.0, 0.0)

    first = lane < 64.0
    picks = []
    for g in range(4):
        picks.append(jnp.where(first, counts[g], 0.0))
        picks.append(jnp.where(first, 0.0, counts[g]))
    picks = jnp.concatenate(picks, axis=0).astype(BF16)
    sums = dot(picks, jnp.concatenate([moments, moments], axis=0))
    high, low = split(sums)

    wide = moments.astype(F32)
    upper = jnp.zeros((8, 256), F32)
    for i in range(8):
        upper = upper + dot_nt(wide[8 * i : 8 * i + 8].astype(BF16), upward[i])
    upper = upper.astype(BF16)

    far = jnp.zeros((64, 256), F32)
    moved = []
    for o in range(8):
        both = jnp.concatenate([high[64 * o : 64 * o + 64], low[64 * o : 64 * o + 64]], axis=0)
        part = dot_nt(both, transfer[o])
        far = far + part[0:64] + part[64:128]
        moved.append(dot_nt(upper, transfer[o]))
    moved_high, moved_low = split(jnp.concatenate(moved, axis=0))
    weights = parent_counts[:, 0:64].astype(BF16)
    coarse = dot(weights, moved_high) + dot(weights, moved_low)
    coarse = coarse.astype(BF16).astype(F32)
    down = [dot_nt(coarse[8 * j : 8 * j + 8].astype(BF16), shift[j]) for j in range(8)]
    local = (far + jnp.concatenate(down, axis=0)).astype(BF16)

    rows, cols = iota((512, 128), 0), iota((512, 128), 1)
    cell = (cols & 7) * 8 + ((cols >> 3) & 7)
    spread = jnp.where(((rows >> 3) == cell) & ((rows & 1) == (cols >> 6)), 1.0, 0.0).astype(BF16)
    out[...] = dot(spread, jnp.concatenate([local[:, 0:128], local[:, 128:256]], axis=0)).astype(BF16)


def gather_near(first, sources, counts, buffers, mats, window, chosen, slots, valid, blocks, sems, mat_sem):
    copies = [
        pltpu.make_async_copy(buffer, window.at[pl.ds(n * 12, 12)], sems.at[n]) for n, buffer in enumerate(buffers)
    ]
    for copy in copies:
        copy.start()
    last = first + 12 * len(buffers)

    level, odd_leaf = lax.axis_index("level"), lax.axis_index("leaf") & 1

    def place(source):
        subtree = jnp.where(source >= 48, 1, 0) + jnp.where(source >= 96, 1, 0)
        block = source - 48 * subtree
        quarter = (block * 43) >> 9
        is_inner = (subtree == 0) == (odd_leaf == 1)
        group = jnp.where(subtree == 1, 0, jnp.where(is_inner, 1, 2))
        at = group * 4 + ((quarter - level) & 3)
        at = jnp.where(at == 6, 8, jnp.where((at == 7) | (at == 8), at - 1, at))
        return at * 12 + block - 12 * quarter

    def take(b, k, n):
        source = place(sources[b, k])
        mine = (source >= first) & (source < last)

        @pl.when(mine)
        def _():
            pltpu.make_async_copy(mats.at[b, k], chosen.at[n], mat_sem).start()
            slots[n] = source - first
            valid[n] = 1
            blocks[n >> 1] = b

        return jnp.where(mine, n + 1, n)

    def take_block(b, state):
        n, used = state
        end = lax.fori_loop(0, counts[b], functools.partial(take, b), n)
        odd = (end - n) & 1

        @pl.when(odd == 1)
        def _():
            slots[end] = 0
            valid[end] = 0

        return end + odd, used + end - n

    n, used = lax.fori_loop(0, counts.shape[0], take_block, (jnp.int32(0), jnp.int32(0)))
    for extra in range(2 * GROUP):
        slots[n + extra] = 0
        valid[n + extra] = 0
        blocks[(n + extra) >> 1] = 0

    def wait(_, x):
        pltpu.make_async_copy(mats.at[0, 0], chosen.at[0], mat_sem).wait()
        return x

    lax.fori_loop(0, used, wait, 0)
    for copy in copies:
        copy.wait()
    return (n + 2 * GROUP - 1) // (2 * GROUP)


def multiply_near(steps, window, chosen, slots, valid, blocks, total):
    def step(i, x):
        parts = []
        for u in range(GROUP):
            at = (i * GROUP + u) * 2
            left = [jnp.where(valid[at + h] == 1, chosen[at + h], 0).astype(BF16) for h in range(2)]
            right = [window[slots[at + h]] for h in range(2)]
            parts.append(dot(jnp.concatenate(left, axis=1), jnp.concatenate(right, axis=0)))
        for u in range(GROUP):
            b = blocks[i * GROUP + u]
            total[b] = total[b] + parts[u]
        return x

    lax.fori_loop(0, steps, step, 0)


def near_kernel(sources, counts, *refs):
    buffers, (mats, out, *scratch) = refs[:-9], refs[-9:]
    window, chosen, slots, valid, blocks, sems, mat_sem = scratch
    steps = gather_near(0, sources, counts, buffers, mats, window, chosen, slots, valid, blocks, sems, mat_sem)
    out[...] = jnp.zeros_like(out)
    multiply_near(steps, window, chosen, slots, valid, blocks, out)


def last_kernel(first, sources, counts, *refs):
    buffers, (mats, near, evals, local, out, spread, turned, *scratch) = refs[:-14], refs[-14:]
    window, chosen, slots, valid, blocks, sems, mat_sem = scratch
    steps = gather_near(first, sources, counts, buffers, mats, window, chosen, slots, valid, blocks, sems, mat_sem)
    spread[...] = local[...].astype(F32)
    for j in range(2):
        turned[128 * j : 128 * j + 128, :] = spread[pl.ds(j, 256, stride=2), :].T.astype(BF16)
    for b in range(0, near.shape[0], 2):
        far = dot(evals[b : b + 2].reshape(256, 256), turned[...])
        out[b : b + 2] = near[b : b + 2] + far.reshape(2, 128, 256)
    multiply_near(steps, window, chosen, slots, valid, blocks, out)


def call_moment(charges, maps, lists, weights):
    vmem, hbm = pl.BlockSpec(memory_space=pltpu.VMEM), pl.BlockSpec(memory_space=pltpu.HBM)
    return pl.pallas_call(
        moment_kernel,
        out_shape=[jax.ShapeDtypeStruct((1024, 128), BF16)] + [pltpu.VMEM(w.shape, BF16) for w in weights],
        in_specs=[vmem] * (2 + len(lists)) + [hbm] * len(weights),
        out_specs=[vmem] * (1 + len(weights)),
        scratch_shapes=[pltpu.VMEM((8, 128), F32), pltpu.VMEM((1024, 128), F32), pltpu.SemaphoreType.DMA((3,))],
        compiler_params=pltpu.CompilerParams(vmem_limit_bytes=56 << 20),
        name="moment",
    )(charges, maps, *lists, *weights)


def call_far(received, weights):
    return pl.pallas_call(
        far_kernel,
        out_shape=jax.ShapeDtypeStruct((512, 128), BF16),
        in_specs=[pl.BlockSpec(memory_space=pltpu.VMEM)] * (1 + len(weights)),
        out_specs=pl.BlockSpec(memory_space=pltpu.VMEM),
        compiler_params=pltpu.CompilerParams(vmem_limit_bytes=24 << 20),
        name="far",
    )(received, *weights)


def near_scratch(buffers):
    return [
        pltpu.VMEM((12 * len(buffers), 128, 256), BF16),
        pltpu.VMEM((192 + 2 * GROUP, 128, 128), BF16),
        pltpu.SMEM((192 + 2 * GROUP,), jnp.int32),
        pltpu.SMEM((192 + 2 * GROUP,), jnp.int32),
        pltpu.SMEM((96 + GROUP,), jnp.int32),
        pltpu.SemaphoreType.DMA((len(buffers),)),
        pltpu.SemaphoreType.DMA,
    ]


def call_near(sources, counts, buffers, mats):
    smem, vmem, hbm = (pl.BlockSpec(memory_space=m) for m in (pltpu.SMEM, pltpu.VMEM, pltpu.HBM))
    return pl.pallas_call(
        near_kernel,
        out_shape=jax.ShapeDtypeStruct((mats.shape[0], 128, 256), F32),
        in_specs=[smem, smem] + [hbm] * (len(buffers) + 1),
        out_specs=vmem,
        scratch_shapes=near_scratch(buffers),
        compiler_params=pltpu.CompilerParams(vmem_limit_bytes=58 << 20),
        name="near",
    )(sources, counts, *buffers, mats)


def call_last(sources, counts, buffers, mats, near, evals, local):
    smem, vmem, hbm = (pl.BlockSpec(memory_space=m) for m in (pltpu.SMEM, pltpu.VMEM, pltpu.HBM))
    return pl.pallas_call(
        functools.partial(last_kernel, 144 - 12 * len(buffers)),
        out_shape=jax.ShapeDtypeStruct((mats.shape[0], 128, 256), F32),
        in_specs=[smem, smem] + [hbm] * (len(buffers) + 1) + [vmem] * 3,
        out_specs=vmem,
        scratch_shapes=[pltpu.VMEM((512, 128), F32), pltpu.VMEM((256, 256), BF16)] + near_scratch(buffers),
        compiler_params=pltpu.CompilerParams(vmem_limit_bytes=24 << 20),
        name="last",
    )(sources, counts, *buffers, mats, near, evals, local)


def flat(pairs):
    return [(a * 4 + b, c * 4 + d) for (a, b), (c, d) in pairs]


def outer(leaf):
    return leaf + 1 if leaf % 2 else leaf - 1


def outer_pairs(leaves, turn):
    return flat(
        [
            ((leaf, y), (outer(leaf), (y + turn) % 4))
            for leaf in range(leaves)
            for y in range(4)
            if 0 <= outer(leaf) < leaves
        ]
    )


def inner_pairs(leaves):
    return flat([((leaf, y), (leaf ^ 1, y)) for leaf in range(leaves) for y in range(4)])


def on_device(
    charges,
    near_mat,
    near_source,
    near_count,
    moment_map,
    local_eval,
    upward_child_translation,
    shift_down,
    transfer_ops,
    subtree_interaction_list,
    subtree_interaction_operators,
    parent_list,
    parent_ops,
):
    leaves = lax.axis_size("leaf")
    ring = [(i, (i + 1) % 4) for i in range(4)]
    back = [((i + 1) % 4, i) for i in range(4)]
    inner = inner_pairs(leaves)

    below = lax.ppermute(charges, "level", ring)
    above = lax.ppermute(charges, "level", back)
    outer_own = lax.ppermute(charges, BOTH, outer_pairs(leaves, 0))
    inner_own = lax.ppermute(charges, BOTH, inner)

    lists = (subtree_interaction_list, subtree_interaction_operators, parent_list, parent_ops)
    message, *weights = call_moment(charges, moment_map, lists, (upward_child_translation, transfer_ops, shift_down))
    received = lax.all_to_all(message.reshape(256, 4, 128), BOTH, 0, 0, tiled=True).reshape(1024, 128)

    outer_below = lax.ppermute(below, BOTH, outer_pairs(leaves, 0))
    outer_above = lax.ppermute(above, BOTH, outer_pairs(leaves, 0))
    far_own = lax.ppermute(below, "level", ring)
    outer_far = lax.ppermute(above, BOTH, outer_pairs(leaves, -1))
    inner_below = lax.ppermute(below, BOTH, inner)
    inner_above = lax.ppermute(above, BOTH, inner)

    columns = call_far(received, weights)
    inner_far = lax.ppermute(far_own, BOTH, inner)

    local = lax.all_to_all(columns.reshape(256, 2, 128), BOTH, 0, 0, tiled=True).reshape(512, 128)

    near_mat = pltpu.with_memory_space_constraint(near_mat, pltpu.HBM)
    early = [charges, above, far_own, below, inner_own, inner_above, inner_below, outer_own]
    late = [inner_far, outer_above, outer_far, outer_below]
    near = call_near(near_source, near_count, early, near_mat)
    return call_last(near_source, near_count, late, near_mat, near, local_eval, local)


def solution(mesh):
    placed = (
        P(("leaf", "level"), None, None),
        P(("leaf", "level"), None, None, None),
        P(("leaf", "level"), None),
        P(("leaf", "level")),
        P(("leaf", "level"), None, None),
        P(("leaf", "level"), None, None),
        P(),
        P(),
        P(),
        P("leaf", None),
        P("leaf", None),
        P("leaf", None),
        P("leaf", None),
    )
    return jax.shard_map(
        on_device,
        mesh=mesh,
        in_specs=placed,
        out_specs=P(("leaf", "level"), None, None),
        check_vma=False,
    )
```

```python
import functools

import jax
import jax.numpy as jnp
from jax import lax
from jax.experimental import pallas as pl
from jax.experimental.pallas import tpu as pltpu
from jax.sharding import PartitionSpec as P


BOTH = ("leaf", "level")
NT = (((1,), (1,)), ((), ()))
F32 = jnp.float32
BF16 = jnp.bfloat16
GROUP = 4


def dot(a, b):
    return jnp.dot(a, b, preferred_element_type=F32)


def dot_nt(a, b):
    return lax.dot_general(a, b, NT, preferred_element_type=F32)


def moment_kernel(charges, maps, cells, ops, parents, parent_ops, out, row, spread):
    blocks = charges.shape[0]
    total = None
    for b in range(0, blocks, 2):
        left = jnp.concatenate([maps[b], maps[b + 1]], axis=1)
        right = jnp.concatenate([charges[b], charges[b + 1]], axis=0)
        part = dot(left, right)
        total = part if total is None else total + part
    turned = total.T
    row[...] = jnp.zeros_like(row)
    row[0:1, 0:32] = ((cells[...] & 7) * 8 + (cells[...] >> 3)).astype(F32)
    row[0:1, 32:64] = ops[...].astype(F32)
    row[0:1, 64:72] = parents[...].astype(F32)
    row[0:1, 72:80] = parent_ops[...].astype(F32)
    for j in range(2):
        spread[pl.ds(j, 256, stride=4), :] = turned[:, 128 * j : 128 * j + 128]
    spread[pl.ds(2, 256, stride=4), :] = jnp.broadcast_to(row[0:1, :], (256, 128))
    spread[pl.ds(3, 256, stride=4), :] = jnp.zeros((256, 128), F32)
    out[...] = spread[...].astype(BF16)


def iota(shape, dim):
    return lax.broadcasted_iota(jnp.int32, shape, dim)


def split(x):
    high = x.astype(BF16)
    return high, (x - high.astype(F32)).astype(BF16)


def far_kernel(received, upward, transfer, shift_hbm, out, shift, sem):
    copy = pltpu.make_async_copy(shift_hbm, shift, sem)
    copy.start()
    rows, cols = iota((64, 1024), 0), iota((64, 1024), 1)
    cell = (rows & 7) * 8 + (rows >> 3)
    chosen = []
    for j in range(2):
        chosen.append(jnp.where(((cols >> 4) == cell) & ((cols & 3) == j), 1.0, 0.0))
    chosen.append(jnp.where(cols == cell * 16 + 2, 1.0, 0.0))
    gathered = dot(jnp.concatenate(chosen, axis=0).astype(BF16), received[...])
    moments = jnp.concatenate([gathered[0:64], gathered[64:128]], axis=1).astype(BF16)
    lists = gathered[128:192]
    lane = iota((64, 128), 1).astype(F32)

    codes = lists[:, 32:64] * 64.0 + lists[:, 0:32]
    counts = [jnp.zeros((64, 128), F32) for _ in range(4)]
    for k in range(32):
        code = jnp.broadcast_to(codes[:, k : k + 1], (64, 128)) - lane
        for g in range(4):
            counts[g] = counts[g] + jnp.where(code == 128.0 * g, 1.0, 0.0)
    parent_codes = lists[:, 72:80] * 8.0 + lists[:, 64:72]
    parent_counts = jnp.zeros((64, 128), F32)
    for k in range(8):
        code = jnp.broadcast_to(parent_codes[:, k : k + 1], (64, 128))
        parent_counts = parent_counts + jnp.where(code == lane, 1.0, 0.0)

    first = lane < 64.0
    picks = []
    for g in range(4):
        picks.append(jnp.where(first, counts[g], 0.0))
        picks.append(jnp.where(first, 0.0, counts[g]))
    picks = jnp.concatenate(picks, axis=0).astype(BF16)
    sums = dot(picks, jnp.concatenate([moments, moments], axis=0))
    high, low = split(sums)

    copy.wait()
    wide = moments.astype(F32)
    upper = jnp.zeros((8, 256), F32)
    for i in range(8):
        upper = upper + dot_nt(wide[8 * i : 8 * i + 8].astype(BF16), upward[i])
    upper = upper.astype(BF16)

    far = jnp.zeros((64, 256), F32)
    moved = []
    for o in range(8):
        both = jnp.concatenate([high[64 * o : 64 * o + 64], low[64 * o : 64 * o + 64]], axis=0)
        part = dot_nt(both, transfer[o])
        far = far + part[0:64] + part[64:128]
        moved.append(dot_nt(upper, transfer[o]))
    moved_high, moved_low = split(jnp.concatenate(moved, axis=0))
    weights = parent_counts[:, 0:64].astype(BF16)
    coarse = dot(weights, moved_high) + dot(weights, moved_low)
    coarse = coarse.astype(BF16).astype(F32)
    down = [dot_nt(coarse[8 * j : 8 * j + 8].astype(BF16), shift[j]) for j in range(8)]
    local = (far + jnp.concatenate(down, axis=0)).astype(BF16)

    rows, cols = iota((512, 128), 0), iota((512, 128), 1)
    cell = (cols & 7) * 8 + ((cols >> 3) & 7)
    spread = jnp.where(((rows >> 3) == cell) & ((rows & 1) == (cols >> 6)), 1.0, 0.0).astype(BF16)
    out[...] = dot(spread, jnp.concatenate([local[:, 0:128], local[:, 128:256]], axis=0)).astype(BF16)


def list_near(early, sources, counts, mats, lists, chosen, sem):
    level, odd_leaf = lax.axis_index("level"), lax.axis_index("leaf") & 1

    def place(source):
        subtree = jnp.where(source >= 48, 1, 0) + jnp.where(source >= 96, 1, 0)
        block = source - 48 * subtree
        quarter = (block * 43) >> 9
        is_inner = (subtree == 0) == (odd_leaf == 1)
        group = jnp.where(subtree == 1, 0, jnp.where(is_inner, 1, 2))
        at = group * 4 + ((quarter - level) & 3)
        at = jnp.where(at == 6, 8, jnp.where((at == 7) | (at == 8), at - 1, at))
        return at * 12 + block - 12 * quarter

    def add(which, source, b, k, n):
        if which == 0:
            pltpu.make_async_copy(mats.at[b, k], chosen.at[n], sem).start()
        lists[which][0, n] = source
        lists[which][1, n] = k + 1
        lists[which][2, n >> 1] = b

    def take(b, k, state):
        n0, n1 = state
        source = place(sources[b, k])
        is_late = source >= early

        @pl.when(is_late)
        def _():
            add(1, source - early, b, k, n1)

        @pl.when(jnp.logical_not(is_late))
        def _():
            add(0, source, b, k, n0)

        step = jnp.where(is_late, 1, 0)
        return n0 + 1 - step, n1 + step

    def take_block(b, state):
        starts, used = state[0:2], state[2:4]
        ends = lax.fori_loop(0, counts[b], functools.partial(take, b), starts)
        odd = [(end - start) & 1 for end, start in zip(ends, starts)]
        for which in range(2):

            @pl.when(odd[which] == 1)
            def _():
                lists[which][0, ends[which]] = 0
                lists[which][1, ends[which]] = 0

        used = tuple(u + end - start for u, end, start in zip(used, ends, starts))
        return tuple(end + o for end, o in zip(ends, odd)) + used

    state = lax.fori_loop(0, counts.shape[0], take_block, (jnp.int32(0),) * 4)
    for which in range(2):
        n = state[which]
        for extra in range(2 * GROUP):
            lists[which][0, n + extra] = 0
            lists[which][1, n + extra] = 0
            lists[which][2, (n + extra) >> 1] = 0
        lists[which][2, 255] = (n + 2 * GROUP - 1) // (2 * GROUP)
    return state[2]


def wait_chosen(used, mats, chosen, sem):
    def wait(_, x):
        pltpu.make_async_copy(mats.at[0, 0], chosen.at[0], sem).wait()
        return x

    lax.fori_loop(0, used, wait, 0)


def multiply_near(window, chosen, listed, total):
    def step(i, x):
        parts = []
        for u in range(GROUP):
            at = (i * GROUP + u) * 2
            left = [jnp.where(listed[1, at + h] > 0, chosen[at + h], 0).astype(BF16) for h in range(2)]
            right = [window[listed[0, at + h]] for h in range(2)]
            parts.append(dot(jnp.concatenate(left, axis=1), jnp.concatenate(right, axis=0)))
        for u in range(GROUP):
            b = listed[2, i * GROUP + u]
            total[b] = total[b] + parts[u]
        return x

    lax.fori_loop(0, listed[2, 255], step, 0)


def window_copies(buffers, window, sems):
    return [pltpu.make_async_copy(x, window.at[pl.ds(n * 12, 12)], sems.at[n]) for n, x in enumerate(buffers)]


def near_kernel(sources, counts, *refs):
    buffers, (mats, out, late, window, chosen, listed, sems, mat_sem) = refs[:-8], refs[-8:]
    copies = window_copies(buffers, window, sems)
    for copy in copies:
        copy.start()
    used = list_near(12 * len(buffers), sources, counts, mats, (listed, late), chosen, mat_sem)
    out[...] = jnp.zeros_like(out)
    wait_chosen(used, mats, chosen, mat_sem)
    for copy in copies:
        copy.wait()
    multiply_near(window, chosen, listed, out)


def last_kernel(late, *refs):
    buffers, (mats, near, evals, local, out, spread, turned, window, chosen, sems, mat_sem) = refs[:-11], refs[-11:]
    copies = window_copies(buffers, window, sems)
    for copy in copies:
        copy.start()

    def take(n, used):
        k = late[1, n]

        @pl.when(k > 0)
        def _():
            pltpu.make_async_copy(mats.at[late[2, n >> 1], k - 1], chosen.at[n], mat_sem).start()

        return used + jnp.where(k > 0, 1, 0)

    used = lax.fori_loop(0, late[2, 255] * 2 * GROUP, take, jnp.int32(0))
    spread[...] = local[...].astype(F32)
    for j in range(2):
        turned[128 * j : 128 * j + 128, :] = spread[pl.ds(j, 256, stride=2), :].T.astype(BF16)
    for b in range(0, near.shape[0], 2):
        far = dot(evals[b : b + 2].reshape(256, 256), turned[...])
        out[b : b + 2] = near[b : b + 2] + far.reshape(2, 128, 256)
    wait_chosen(used, mats, chosen, mat_sem)
    for copy in copies:
        copy.wait()
    multiply_near(window, chosen, late, out)


def call_moment(charges, maps, lists):
    vmem = pl.BlockSpec(memory_space=pltpu.VMEM)
    return pl.pallas_call(
        moment_kernel,
        out_shape=jax.ShapeDtypeStruct((1024, 128), BF16),
        in_specs=[vmem] * (2 + len(lists)),
        out_specs=vmem,
        scratch_shapes=[pltpu.VMEM((8, 128), F32), pltpu.VMEM((1024, 128), F32)],
        compiler_params=pltpu.CompilerParams(vmem_limit_bytes=58 << 20),
        name="moment",
    )(charges, maps, *lists)


def call_far(received, weights):
    return pl.pallas_call(
        far_kernel,
        out_shape=jax.ShapeDtypeStruct((512, 128), BF16),
        in_specs=[VMEM] * 3 + [HBM],
        out_specs=VMEM,
        scratch_shapes=[pltpu.VMEM(weights[2].shape, BF16), pltpu.SemaphoreType.DMA],
        compiler_params=pltpu.CompilerParams(vmem_limit_bytes=24 << 20),
        name="far",
    )(received, *weights)


SLOTS = 192 + 2 * GROUP
SMEM, VMEM, HBM = (pl.BlockSpec(memory_space=m) for m in (pltpu.SMEM, pltpu.VMEM, pltpu.HBM))


def call_near(sources, counts, buffers, mats):
    return pl.pallas_call(
        near_kernel,
        out_shape=[pltpu.VMEM((mats.shape[0], 128, 256), F32), jax.ShapeDtypeStruct((3, 256), jnp.int32)],
        in_specs=[SMEM, SMEM] + [HBM] * (len(buffers) + 1),
        out_specs=[VMEM, SMEM],
        scratch_shapes=[
            pltpu.VMEM((12 * len(buffers), 128, 256), BF16),
            pltpu.VMEM((SLOTS, 128, 128), BF16),
            pltpu.SMEM((3, 256), jnp.int32),
            pltpu.SemaphoreType.DMA((len(buffers),)),
            pltpu.SemaphoreType.DMA,
        ],
        compiler_params=pltpu.CompilerParams(vmem_limit_bytes=58 << 20),
        name="near",
    )(sources, counts, *buffers, mats)


def call_last(late, buffers, mats, near, evals, local):
    return pl.pallas_call(
        last_kernel,
        out_shape=jax.ShapeDtypeStruct(near.shape, F32),
        in_specs=[SMEM] + [HBM] * (len(buffers) + 1) + [VMEM] * 3,
        out_specs=VMEM,
        scratch_shapes=[
            pltpu.VMEM((512, 128), F32),
            pltpu.VMEM((256, 256), BF16),
            pltpu.VMEM((12 * len(buffers), 128, 256), BF16),
            pltpu.VMEM((SLOTS, 128, 128), BF16),
            pltpu.SemaphoreType.DMA((len(buffers),)),
            pltpu.SemaphoreType.DMA,
        ],
        compiler_params=pltpu.CompilerParams(vmem_limit_bytes=24 << 20),
        name="last",
    )(late, *buffers, mats, near, evals, local)


def permute(x, axes, pairs):
    return pltpu.with_memory_space_constraint(lax.ppermute(x, axes, pairs), pltpu.HBM)


def flat(pairs):
    return [(a * 4 + b, c * 4 + d) for (a, b), (c, d) in pairs]


def outer(leaf):
    return leaf + 1 if leaf % 2 else leaf - 1


def outer_pairs(leaves, turn):
    return flat(
        [
            ((leaf, y), (outer(leaf), (y + turn) % 4))
            for leaf in range(leaves)
            for y in range(4)
            if 0 <= outer(leaf) < leaves
        ]
    )


def inner_pairs(leaves):
    return flat([((leaf, y), (leaf ^ 1, y)) for leaf in range(leaves) for y in range(4)])


def on_device(
    charges,
    near_mat,
    near_source,
    near_count,
    moment_map,
    local_eval,
    upward_child_translation,
    shift_down,
    transfer_ops,
    subtree_interaction_list,
    subtree_interaction_operators,
    parent_list,
    parent_ops,
):
    leaves = lax.axis_size("leaf")
    ring = [(i, (i + 1) % 4) for i in range(4)]
    back = [((i + 1) % 4, i) for i in range(4)]
    inner = inner_pairs(leaves)

    below = permute(charges, "level", ring)
    above = permute(charges, "level", back)
    outer_own = permute(charges, BOTH, outer_pairs(leaves, 0))
    inner_own = permute(charges, BOTH, inner)

    lists = (subtree_interaction_list, subtree_interaction_operators, parent_list, parent_ops)
    message = call_moment(charges, moment_map, lists)
    shift_down = pltpu.with_memory_space_constraint(shift_down, pltpu.HBM)
    weights = (upward_child_translation, transfer_ops, shift_down)
    received = lax.all_to_all(message.reshape(256, 4, 128), BOTH, 0, 0, tiled=True).reshape(1024, 128)

    outer_below = permute(below, BOTH, outer_pairs(leaves, 0))
    outer_above = permute(above, BOTH, outer_pairs(leaves, 0))
    far_own = permute(below, "level", ring)
    outer_far = permute(above, BOTH, outer_pairs(leaves, -1))
    inner_below = permute(below, BOTH, inner)
    inner_above = permute(above, BOTH, inner)

    columns = call_far(received, weights)
    inner_far = permute(far_own, BOTH, inner)

    local = lax.all_to_all(columns.reshape(256, 2, 128), BOTH, 0, 0, tiled=True).reshape(512, 128)

    near_mat = pltpu.with_memory_space_constraint(near_mat, pltpu.HBM)
    early = [charges, above, far_own, below, inner_own, inner_above, inner_below, outer_own]
    late = [inner_far, outer_above, outer_far, outer_below]
    near, listed = call_near(near_source, near_count, early, near_mat)
    listed = pltpu.with_memory_space_constraint(listed, pltpu.HBM)
    return call_last(listed, late, near_mat, near, local_eval, local)


def solution(mesh):
    placed = (
        P(("leaf", "level"), None, None),
        P(("leaf", "level"), None, None, None),
        P(("leaf", "level"), None),
        P(("leaf", "level")),
        P(("leaf", "level"), None, None),
        P(("leaf", "level"), None, None),
        P(),
        P(),
        P(),
        P("leaf", None),
        P("leaf", None),
        P("leaf", None),
        P("leaf", None),
    )
    return jax.shard_map(
        on_device,
        mesh=mesh,
        in_specs=placed,
        out_specs=P(("leaf", "level"), None, None),
        check_vma=False,
    )
```
